512 devices in a mesh: tm: 128 (over x_lo, z, y), feat: 4 (over x_hi, core).
Axes of the slice: x: 4 (x_hi: 2, x_lo: 2; x = x_hi * 2 + x_lo), y: 4, z: 16, core: 2. Of those that a mesh axis runs over, the one named last changes fastest.
Arguments:
- frames: bfloat16 [4096, 2048], P('tm'), may hold values from -6 to 6
- frequency: bfloat16 [2048, 4096], P(None, 'feat'), may hold values from -0.125 to 0.125
- phases: float32 [4096], P('feat'), may hold values from -3.140625 to 3.140625
Outputs:
- instant_tiles: float32 [128, 4, 128, 256], P('tm', 'feat')
- lagged_tiles: float32 [128, 4, 128, 256], P('tm', 'feat')
The draws below stay inside these ranges and needn't reach their ends.
All inputs are finite; a program needn't handle non-finite values.
Results may differ from the reference program's by a relative error of at most 0.0003.
Values may be sent and summed in bfloat16 or wider, within the bound.
A program may use at most 64 MiB of HBM per device.

```python
import math
import jax
import jax.numpy as jnp
from jax import lax

DIST = 2048
RF = 4096
LAG = 512
ROW_SPLIT = 8
FRAMES = 4096
TILE_ROWS = 128
TILE_COLS = 256
N_TM = 128
N_FEAT = 4


def shard_levels(rng, dims, pieces, least, top_value):
    def one(dim, blocks):
        draws = jax.random.uniform(jax.random.fold_in(jax.random.fold_in(rng, 6), dim), (blocks,), jnp.float32, least / len(pieces), top_value / len(pieces))
        return jnp.repeat(jnp.exp(draws), dims[dim] // blocks).reshape((-1,) + (1,) * (len(dims) - dim - 1))

    level = one(*pieces[0])
    for cut in pieces[1:]:
        level = level * one(*cut)
    return level


def normal_values(own_key, shape, spread, most, shards=(), held_as=jnp.bfloat16):
    entries = jax.random.normal(own_key, shape, jnp.float32) * spread
    if len(shards) > 0:
        entries = shard_levels(own_key, shape, shards, -0.22, 0.18) * entries
    return jnp.clip(entries, min=-most, max=most).astype(held_as)


def setup_inputs(seed: int = 0) -> dict:
    arg_keys = jax.random.split(jax.random.key(seed), 4)
    frames = normal_values(arg_keys[0], (FRAMES, DIST), 1.0, 6.0, ((0, 128),))
    frequency = normal_values(arg_keys[1], (DIST, RF), DIST ** -0.5, 0.125, ((1, 4),))
    phases = jnp.clip(jax.random.uniform(arg_keys[2], (RF,), jnp.float32, -3.140625, 3.140625), -3.140625, 3.140625)
    return {"frames": frames, "frequency": frequency, "phases": phases}


SCALE = math.sqrt(2.0)

def to_tiles(matrix):
    shaped = matrix.reshape(N_FEAT, ROW_SPLIT, TILE_ROWS, N_TM // ROW_SPLIT, TILE_COLS)
    return shaped.transpose(3, 1, 0, 2, 4).reshape(N_TM, N_FEAT, TILE_ROWS, TILE_COLS)

def reference(frames, frequency, phases):
    projected = jnp.dot(frames, frequency, preferred_element_type=jnp.float32) + phases[None, :]
    rounded = (SCALE * jnp.cos(projected)).astype(jnp.bfloat16)
    rounded = lax.optimization_barrier(rounded)
    features = rounded.astype(jnp.float32)
    instant = jnp.dot(features.T, features, precision=lax.Precision.HIGHEST) / FRAMES
    lagged = jnp.dot(features[:FRAMES - LAG].T, features[LAG:], precision=lax.Precision.HIGHEST) / (FRAMES - LAG)
    return (to_tiles(instant), to_tiles(lagged))
```

```python
import math

import jax
import jax.numpy as jnp
from jax import lax
from jax.sharding import Mesh, PartitionSpec as P

LAG = 512
SCALE = math.sqrt(2.0)
G, K = 16, 8


def shards(frames, frequency, phases):
    feat_count = lax.axis_size("feat")
    projected = jnp.dot(frames, frequency, preferred_element_type=jnp.float32) + phases[None, :]
    feats = (SCALE * jnp.cos(projected)).astype(jnp.bfloat16)
    count, width = feats.shape
    rows = width // K
    cols = width * feat_count // G
    total = count * G * K
    part = count // feat_count
    r = feats.reshape(count, K, rows).transpose(1, 0, 2)
    r = lax.all_to_all(r, "k", split_axis=0, concat_axis=0, tiled=True)
    r = lax.all_gather(r.reshape(K * count, rows), "g", axis=0, tiled=False)
    c = feats.reshape(feat_count, part, width)
    c = lax.all_to_all(c, "feat", split_axis=0, concat_axis=0, tiled=True)
    c = c.reshape(feat_count, part, G // feat_count, cols).transpose(0, 2, 1, 3)
    c = c.reshape(G, part, cols)
    c = lax.all_to_all(c, "g", split_axis=0, concat_axis=0, tiled=True)
    c = lax.all_gather(c, ("k", "feat"), axis=1, tiled=False)
    c = c.reshape(total, cols)
    r = r.reshape(total, rows)
    instant = jnp.einsum("sr,sc->rc", r, c, preferred_element_type=jnp.float32) / total
    lagged = jnp.einsum(
        "sr,sc->rc", r[: total - LAG], c[LAG:], preferred_element_type=jnp.float32
    ) / (total - LAG)
    return instant.reshape(1, 1, rows, cols), lagged.reshape(1, 1, rows, cols)


def solution(mesh):
    fine = Mesh(mesh.devices.reshape(G, K, mesh.shape["feat"]), ("g", "k", "feat"))
    tm = ("g", "k")
    return jax.shard_map(
        shards,
        mesh=fine,
        in_specs=(P(tm, None), P(None, "feat"), P("feat")),
        out_specs=(P(tm, "feat", None, None), P(tm, "feat", None, None)),
        check_vma=False,
    )
```

```python
import math

import jax
import jax.numpy as jnp
from jax import lax
from jax.experimental import pallas as pl
from jax.experimental.pallas import tpu as pltpu
from jax.sharding import Mesh, PartitionSpec as P

SCALE = math.sqrt(2.0)
MESH = pl.DeviceIdType.MESH
AXES = ("xl", "zz", "zp", "y", "xh", "co")
SHAPE = (2, 8, 2, 4, 2, 2)
FRAMES, LAG = 4096, 512
NSEND = 40


def kernel(feats, inst, lagd, rows, cols, send, rsem, zsem, xsem, csem, ysem, osem):
    xl, zz, zp, y, xh, co = (lax.axis_index(a) for a in AXES)
    par, zq, up = zz % 2, zz // 2, zz // 4
    me_k = zp * 4 + y
    own = jnp.logical_and(jnp.logical_and(xl == xh, co == par), co == up)
    sends = []

    def remote(src, dst, sem, **dev):
        copy = pltpu.make_async_remote_copy(
            src_ref=src,
            dst_ref=dst,
            send_sem=send.at[len(sends)],
            recv_sem=sem,
            device_id=dev,
            device_id_type=MESH,
        )
        sends.append(copy)
        return copy

    def arrived(ref, sem):
        pltpu.make_async_copy(ref, ref, sem).wait()

    barrier = pltpu.get_barrier_semaphore()

    def greet(**dev):
        pl.semaphore_signal(barrier, inc=1, device_id=dev, device_id_type=MESH)

    for q in range(4):
        @pl.when(jnp.logical_not(jnp.logical_and(own, zq == q)))
        def _():
            greet(xl=xh, xh=xl, zz=2 * q + co, co=up)
    for d in range(1, 8):
        k = (me_k + d) % 8
        greet(zp=k // 4, y=k % 4)
    above, below = (zz + 1) % 8, (zz + 7) % 8
    greet(zz=above)
    greet(zz=below)
    greet(xl=1 - xl)
    greet(xh=1 - xh)
    greet(co=1 - co)
    pl.semaphore_wait(barrier, 16 - own.astype(jnp.int32))

    for k in range(8):
        src = feats.at[:, 128 * k : 128 * (k + 1)]
        dst = rows.at[y, par, xl, zq, zp]
        copy = remote(src, dst, rsem, zp=k // 4, y=k % 4)
        local = pltpu.make_async_copy(src, dst, rsem)
        pl.when(me_k != k)(copy.start)
        pl.when(me_k == k)(local.start)
    for j in range(4):
        src = feats.at[:, 256 * j : 256 * (j + 1)]
        dst = cols.at[y, par, xl, zq, zp]
        mine = jnp.logical_and(own, zz == 4 * co + j)
        copy = remote(src, dst, csem.at[0], xl=xh, xh=xl, zz=4 * co + j, co=par)
        local = pltpu.make_async_copy(src, dst, csem.at[0])
        pl.when(jnp.logical_not(mine))(copy.start)
        pl.when(mine)(local.start)

    def block(z):
        return rows.at[:, z % 2, xl, z // 2]

    def ring(z, sem, **dev):
        remote(block(z), block(z), sem, **dev).start()

    arrived(block(zz), rsem)
    ring(zz, zsem.at[0, 0], zz=above)
    ring(zz, zsem.at[1, 0], zz=below)
    ring(zz, xsem, xl=1 - xl)

    def step(s):
        lo, hi = (zz + 8 - s) % 8, (zz + s) % 8
        arrived(block(lo), zsem.at[0, s - 1])
        if s < 3:
            ring(lo, zsem.at[0, s], zz=above)
        else:
            half = rows.at[0:2, lo % 2, xl, lo // 2]
            remote(half, half, zsem.at[0, s], zz=above).start()
        arrived(block(hi), zsem.at[1, s - 1])
        if s < 3:
            ring(hi, zsem.at[1, s], zz=below)
        else:
            half = rows.at[2:4, hi % 2, xl, hi // 2]
            remote(half, half, zsem.at[1, s], zz=below).start()
        ring(lo, xsem, xl=1 - xl)
        ring(hi, xsem, xl=1 - xl)

    part = cols.at[y, co, xh, :, zp]
    arrived(part, csem.at[0])
    remote(part, part, csem.at[1], xh=1 - xh).start()
    step(1)
    arrived(cols.at[y, co, 1 - xh, :, zp], csem.at[1])
    part = cols.at[y, co, :, :, zp]
    remote(part, part, csem.at[2], zp=1 - zp).start()
    step(2)
    arrived(cols.at[y, co, :, :, 1 - zp], csem.at[2])
    nxt, prv, opp = (y + 1) % 4, (y + 3) % 4, (y + 2) % 4
    for h in range(2):
        up_half, down_half = cols.at[y, co, h], cols.at[y, co, 1 - h]
        remote(up_half, up_half, ysem.at[0, h], y=nxt).start()
        remote(down_half, down_half, ysem.at[1, 1 - h], y=prv).start()

    def other(v):
        remote(cols.at[v, co], cols.at[v, co], osem, co=1 - co).start()

    other(y)
    step(3)
    arrived(cols.at[prv, co, 0], ysem.at[0, 0])
    far = cols.at[prv, co, 0]
    remote(far, far, ysem.at[0, 2], y=nxt).start()
    arrived(cols.at[nxt, co, 1], ysem.at[1, 1])
    far = cols.at[nxt, co, 1]
    remote(far, far, ysem.at[1, 2], y=prv).start()
    last = (zz + 4) % 8
    arrived(rows.at[0:2, last % 2, xl, last // 2], zsem.at[0, 3])
    arrived(rows.at[2:4, last % 2, xl, last // 2], zsem.at[1, 3])
    ring(last, xsem, xl=1 - xl)
    arrived(cols.at[prv, co, 1], ysem.at[0, 1])
    other(prv)
    arrived(cols.at[nxt, co, 0], ysem.at[1, 0])
    other(nxt)
    arrived(cols.at[opp, co, 0], ysem.at[0, 2])
    arrived(cols.at[opp, co, 1], ysem.at[1, 2])
    other(opp)
    arrived(rows.at[:, :, 1 - xl], xsem)
    arrived(cols.at[:, 1 - co], osem)

    over = (((0,), (0,)), ((), ()))

    def body(i, carry):
        total, late = carry
        r = rows[i // 2, i % 2].reshape(512, 128)
        c = cols[i // 2, i % 2].reshape(512, 256)
        total += lax.dot_general(r, c, over, preferred_element_type=jnp.float32)
        late += lax.dot_general(r[:448], c[64:], over, preferred_element_type=jnp.float32)
        return total, late

    zero = jnp.zeros(inst.shape, jnp.float32)
    total, late = lax.fori_loop(0, 8, body, (zero, zero))
    inst[...] = total / FRAMES
    lagd[...] = late / (FRAMES - LAG)

    for k, copy in enumerate(sends[:8]):
        pl.when(me_k != k)(copy.wait_send)
    for j, copy in enumerate(sends[8:12]):
        mine = jnp.logical_and(own, zz == 4 * co + j)
        pl.when(jnp.logical_not(mine))(copy.wait_send)
    for copy in sends[12:]:
        copy.wait_send()


def shards(frames, frequency, phases):
    projected = jnp.dot(frames, frequency, preferred_element_type=jnp.float32) + phases[None, :]
    feats = (SCALE * jnp.cos(projected)).astype(jnp.bfloat16)
    vmem = pl.BlockSpec(memory_space=pltpu.VMEM)
    dma = pltpu.SemaphoreType.DMA
    tile = jax.ShapeDtypeStruct((128, 256), jnp.float32)
    inst, lagd = pl.pallas_call(
        kernel,
        out_shape=(tile, tile),
        in_specs=[vmem],
        out_specs=(vmem, vmem),
        scratch_shapes=[
            pltpu.VMEM((4, 2, 2, 4, 2, 32, 128), jnp.bfloat16),
            pltpu.VMEM((4, 2, 2, 4, 2, 32, 256), jnp.bfloat16),
            dma((NSEND,)),
            dma,
            dma((2, 4)),
            dma,
            dma((3,)),
            dma((2, 3)),
            dma,
        ],
        compiler_params=pltpu.CompilerParams(collective_id=0, has_side_effects=True),
    )(feats)
    return inst[None, None], lagd[None, None]


def solution(mesh):
    fine = Mesh(mesh.devices.reshape(SHAPE), AXES)
    tm, feat = AXES[:4], AXES[4:]
    return jax.shard_map(
        shards,
        mesh=fine,
        in_specs=(P(tm, None), P(None, feat), P(feat)),
        out_specs=(P(tm, feat, None, None), P(tm, feat, None, None)),
        check_vma=False,
    )
```

```python
import math

import jax
import jax.numpy as jnp
from jax import lax
from jax.experimental import pallas as pl
from jax.experimental.pallas import tpu as pltpu
from jax.sharding import Mesh, PartitionSpec as P

SCALE = math.sqrt(2.0)
MESH = pl.DeviceIdType.MESH
AXES = ("xl", "zz", "zp", "y", "xh", "co")
SHAPE = (2, 8, 2, 4, 2, 2)
FRAMES, LAG = 4096, 512
NSEND = 99
VMEM = 24 * 2**20


def kernel(feats, inst, lagd, rows, cols, send, rsem, zsem, xsem, csem, hsem, ysem, osem):
    xl, zz, zp, y, xh, co = (lax.axis_index(a) for a in AXES)
    par, zq, up = zz % 2, zz // 2, zz // 4
    me_k = zp * 4 + y
    own = jnp.logical_and(jnp.logical_and(xl == xh, co == par), co == up)
    sends = []

    def remote(src, dst, sem, **dev):
        copy = pltpu.make_async_remote_copy(
            src_ref=src,
            dst_ref=dst,
            send_sem=send.at[len(sends)],
            recv_sem=sem,
            device_id=dev,
            device_id_type=MESH,
        )
        sends.append(copy)
        return copy

    def arrived(ref, sem):
        pltpu.make_async_copy(ref, ref, sem).wait()

    barrier = pltpu.get_barrier_semaphore()

    def greet(**dev):
        pl.semaphore_signal(barrier, inc=1, device_id=dev, device_id_type=MESH)

    for q in range(4):
        @pl.when(jnp.logical_not(jnp.logical_and(own, zq == q)))
        def _():
            greet(xl=xh, xh=xl, zz=2 * q + co, co=up)
    for d in range(1, 8):
        k = (me_k + d) % 8
        greet(zp=k // 4, y=k % 4)
    above, below = (zz + 1) % 8, (zz + 7) % 8
    greet(zz=above)
    greet(zz=below)
    greet(xl=1 - xl)
    greet(xh=1 - xh)
    greet(co=1 - co)
    pl.semaphore_wait(barrier, 16 - own.astype(jnp.int32))

    for k in range(8):
        src = feats.at[:, 128 * k : 128 * (k + 1)]
        dst = rows.at[y, par, xl, zq, zp]
        copy = remote(src, dst, rsem.at[y], zp=k // 4, y=k % 4)
        local = pltpu.make_async_copy(src, dst, rsem.at[y])
        pl.when(me_k != k)(copy.start)
        pl.when(me_k == k)(local.start)
    for j in range(4):
        src = feats.at[:, 256 * j : 256 * (j + 1)]
        dst = cols.at[y, par, xl, zq, zp]
        mine = jnp.logical_and(own, zz == 4 * co + j)
        copy = remote(src, dst, csem.at[zq], xl=xh, xh=xl, zz=4 * co + j, co=par)
        local = pltpu.make_async_copy(src, dst, csem.at[zq])
        pl.when(jnp.logical_not(mine))(copy.start)
        pl.when(mine)(local.start)

    def push(ref, sem, **dev):
        remote(ref, ref, sem, **dev).start()

    def chunk(z, d):
        return rows.at[(y + d) % 4, z % 2, xl, z // 2]

    def across(z):
        push(rows.at[:, z % 2, xl, z // 2], xsem, xl=1 - xl)

    def row_start():
        for d in range(4):
            v = (y + d) % 4
            arrived(chunk(zz, d), rsem.at[v])
            push(chunk(zz, d), zsem.at[0, 0, d], zz=above)
            push(chunk(zz, d), zsem.at[1, 0, d], zz=below)
        across(zz)

    def row_step(s):
        lo, hi = (zz + 8 - s) % 8, (zz + s) % 8
        for d in range(4):
            arrived(chunk(lo, d), zsem.at[0, s - 1, d])
            if s < 3 or d < 2:
                push(chunk(lo, d), zsem.at[0, s, d], zz=above)
            arrived(chunk(hi, d), zsem.at[1, s - 1, d])
            if s < 3 or d >= 2:
                push(chunk(hi, d), zsem.at[1, s, d], zz=below)
        across(lo)
        across(hi)

    def row_last():
        last = (zz + 4) % 8
        for d in range(4):
            arrived(chunk(last, d), zsem.at[d // 2, 3, d])
            push(chunk(last, d), xsem, xl=1 - xl)

    nxt, prv, opp = (y + 1) % 4, (y + 3) % 4, (y + 2) % 4
    piece = [(zq + d) % 4 for d in (0, 1, 3, 2)]

    def other(v, p):
        push(cols.at[v, co, :, piece[p]], osem, co=1 - co)

    def col_x(p):
        q = piece[p]
        arrived(cols.at[y, co, xh, q, zp], csem.at[q])
        push(cols.at[y, co, xh, q, zp], hsem.at[0, p], xh=1 - xh)

    def col_z(p):
        q = piece[p]
        arrived(cols.at[y, co, 1 - xh, q, zp], hsem.at[0, p])
        push(cols.at[y, co, :, q, zp], hsem.at[1, p], zp=1 - zp)

    def col_y(p):
        q = piece[p]
        arrived(cols.at[y, co, :, q, 1 - zp], hsem.at[1, p])
        for h in range(2):
            push(cols.at[y, co, h, q], ysem.at[0, p, h], y=nxt)
            push(cols.at[y, co, 1 - h, q], ysem.at[1, p, 1 - h], y=prv)
        other(y, p)

    def col_far(p):
        q = piece[p]
        arrived(cols.at[prv, co, 0, q], ysem.at[0, p, 0])
        push(cols.at[prv, co, 0, q], ysem.at[0, p, 2], y=nxt)
        arrived(cols.at[nxt, co, 1, q], ysem.at[1, p, 1])
        push(cols.at[nxt, co, 1, q], ysem.at[1, p, 2], y=prv)
        arrived(cols.at[prv, co, 1, q], ysem.at[0, p, 1])
        other(prv, p)
        arrived(cols.at[nxt, co, 0, q], ysem.at[1, p, 0])
        other(nxt, p)

    def col_last(p):
        q = piece[p]
        arrived(cols.at[opp, co, 0, q], ysem.at[0, p, 2])
        arrived(cols.at[opp, co, 1, q], ysem.at[1, p, 2])
        other(opp, p)

    row_start()
    col_x(0)
    col_x(1)
    col_x(2)
    row_step(1)
    col_z(0)
    col_x(3)
    col_z(1)
    col_z(2)
    col_y(0)
    row_step(2)
    col_z(3)
    col_y(1)
    col_y(2)
    col_far(0)
    row_step(3)
    col_y(3)
    col_far(1)
    col_far(2)
    col_last(0)
    row_last()
    col_far(3)
    for p in range(1, 4):
        col_last(p)
    arrived(rows.at[:, :, 1 - xl], xsem)
    arrived(cols.at[:, 1 - co], osem)

    over = (((0,), (0,)), ((), ()))

    def body(i, carry):
        total, late = carry
        r = rows[i // 2, i % 2].reshape(512, 128)
        c = cols[i // 2, i % 2].reshape(512, 256)
        total += lax.dot_general(r, c, over, preferred_element_type=jnp.float32)
        late += lax.dot_general(r[:448], c[64:], over, preferred_element_type=jnp.float32)
        return total, late

    zero = jnp.zeros(inst.shape, jnp.float32)
    total, late = lax.fori_loop(0, 8, body, (zero, zero))
    inst[...] = total / FRAMES
    lagd[...] = late / (FRAMES - LAG)

    for k, copy in enumerate(sends[:8]):
        pl.when(me_k != k)(copy.wait_send)
    for j, copy in enumerate(sends[8:12]):
        mine = jnp.logical_and(own, zz == 4 * co + j)
        pl.when(jnp.logical_not(mine))(copy.wait_send)
    assert len(sends) == NSEND
    for copy in sends[12:]:
        copy.wait_send()


def shards(frames, frequency, phases):
    projected = jnp.dot(frames, frequency, preferred_element_type=jnp.float32) + phases[None, :]
    feats = (SCALE * jnp.cos(projected)).astype(jnp.bfloat16)
    vmem = pl.BlockSpec(memory_space=pltpu.VMEM)
    dma = pltpu.SemaphoreType.DMA
    tile = jax.ShapeDtypeStruct((128, 256), jnp.float32)
    inst, lagd = pl.pallas_call(
        kernel,
        out_shape=(tile, tile),
        in_specs=[vmem],
        out_specs=(vmem, vmem),
        scratch_shapes=[
            pltpu.VMEM((4, 2, 2, 4, 2, 32, 128), jnp.bfloat16),
            pltpu.VMEM((4, 2, 2, 4, 2, 32, 256), jnp.bfloat16),
            dma((NSEND,)),
            dma((4,)),
            dma((2, 4, 4)),
            dma,
            dma((4,)),
            dma((2, 4)),
            dma((2, 4, 3)),
            dma,
        ],
        compiler_params=pltpu.CompilerParams(collective_id=0, has_side_effects=True, vmem_limit_bytes=VMEM),
    )(feats)
    return inst[None, None], lagd[None, None]


def solution(mesh):
    fine = Mesh(mesh.devices.reshape(SHAPE), AXES)
    tm, feat = AXES[:4], AXES[4:]
    return jax.shard_map(
        shards,
        mesh=fine,
        in_specs=(P(tm, None), P(None, feat), P(feat)),
        out_specs=(P(tm, feat, None, None), P(tm, feat, None, None)),
        check_vma=False,
    )
```

```python
import math

import jax
import jax.numpy as jnp
from jax import lax
from jax.experimental import pallas as pl
from jax.experimental.pallas import tpu as pltpu
from jax.sharding import Mesh, PartitionSpec as P

SCALE = math.sqrt(2.0)
MESH = pl.DeviceIdType.MESH
AXES = ("xl", "zz", "zp", "y", "xh", "co")
SHAPE = (2, 8, 2, 4, 2, 2)
FRAMES, LAG = 4096, 512
NSEND = 99
VMEM = 55_000_000


def kernel(frames, freq, phases, inst, lagd, fbuf, wbuf, feats, ins, rows, cols, send, rsem, zsem, xsem, csem, hsem, ysem, osem):
    xl, zz, zp, y, xh, co = (lax.axis_index(a) for a in AXES)
    par, zq, up = zz % 2, zz // 2, zz // 4
    me_k = zp * 4 + y
    own = jnp.logical_and(jnp.logical_and(xl == xh, co == par), co == up)
    sends = []

    def remote(src, dst, sem, **dev):
        copy = pltpu.make_async_remote_copy(
            src_ref=src,
            dst_ref=dst,
            send_sem=send.at[len(sends)],
            recv_sem=sem,
            device_id=dev,
            device_id_type=MESH,
        )
        sends.append(copy)
        return copy

    def arrived(ref, sem):
        pltpu.make_async_copy(ref, ref, sem).wait()

    barrier = pltpu.get_barrier_semaphore()

    def greet(**dev):
        pl.semaphore_signal(barrier, inc=1, device_id=dev, device_id_type=MESH)

    for q in range(4):
        @pl.when(jnp.logical_not(jnp.logical_and(own, zq == q)))
        def _():
            greet(xl=xh, xh=xl, zz=2 * q + co, co=up)
    for d in range(1, 8):
        k = (me_k + d) % 8
        greet(zp=k // 4, y=k % 4)
    above, below = (zz + 1) % 8, (zz + 7) % 8
    greet(zz=above)
    greet(zz=below)
    greet(xl=1 - xl)
    greet(xh=1 - xh)
    greet(co=1 - co)

    loads = [pltpu.make_async_copy(frames, fbuf, ins.at[4])]
    for j in range(4):
        part = slice(256 * j, 256 * (j + 1))
        loads.append(pltpu.make_async_copy(freq.at[:, part], wbuf.at[:, part], ins.at[j]))
    for load in loads:
        load.start()
    loads[0].wait()
    for j in range(4):
        part = slice(256 * j, 256 * (j + 1))
        loads[1 + j].wait()
        projected = jnp.dot(fbuf[...], wbuf[:, part], preferred_element_type=jnp.float32)
        projected += phases[:, part]
        feats[:, part] = (SCALE * jnp.cos(projected)).astype(jnp.bfloat16)
    pl.semaphore_wait(barrier, 16 - own.astype(jnp.int32))

    for k in range(8):
        src = feats.at[:, 128 * k : 128 * (k + 1)]
        dst = rows.at[y, par, xl, zq, zp]
        copy = remote(src, dst, rsem.at[y], zp=k // 4, y=k % 4)
        local = pltpu.make_async_copy(src, dst, rsem.at[y])
        pl.when(me_k != k)(copy.start)
        pl.when(me_k == k)(local.start)
    for j in range(4):
        src = feats.at[:, 256 * j : 256 * (j + 1)]
        dst = cols.at[y, par, xl, zq, zp]
        mine = jnp.logical_and(own, zz == 4 * co + j)
        copy = remote(src, dst, csem.at[zq], xl=xh, xh=xl, zz=4 * co + j, co=par)
        local = pltpu.make_async_copy(src, dst, csem.at[zq])
        pl.when(jnp.logical_not(mine))(copy.start)
        pl.when(mine)(local.start)

    def push(ref, sem, **dev):
        remote(ref, ref, sem, **dev).start()

    def chunk(z, d):
        return rows.at[(y + d) % 4, z % 2, xl, z // 2]

    def across(z):
        push(rows.at[:, z % 2, xl, z // 2], xsem, xl=1 - xl)

    def row_start():
        for d in range(4):
            v = (y + d) % 4
            arrived(chunk(zz, d), rsem.at[v])
            push(chunk(zz, d), zsem.at[0, 0, d], zz=above)
            push(chunk(zz, d), zsem.at[1, 0, d], zz=below)
        across(zz)

    def row_step(s):
        lo, hi = (zz + 8 - s) % 8, (zz + s) % 8
        for d in range(4):
            arrived(chunk(lo, d), zsem.at[0, s - 1, d])
            if s < 3 or d < 2:
                push(chunk(lo, d), zsem.at[0, s, d], zz=above)
            arrived(chunk(hi, d), zsem.at[1, s - 1, d])
            if s < 3 or d >= 2:
                push(chunk(hi, d), zsem.at[1, s, d], zz=below)
        across(lo)
        across(hi)

    def row_last():
        last = (zz + 4) % 8
        for d in range(4):
            arrived(chunk(last, d), zsem.at[d // 2, 3, d])
            push(chunk(last, d), xsem, xl=1 - xl)

    nxt, prv, opp = (y + 1) % 4, (y + 3) % 4, (y + 2) % 4
    piece = [(zq + d) % 4 for d in (0, 1, 3, 2)]

    def other(v, p):
        push(cols.at[v, co, :, piece[p]], osem, co=1 - co)

    def col_x(p):
        q = piece[p]
        arrived(cols.at[y, co, xh, q, zp], csem.at[q])
        push(cols.at[y, co, xh, q, zp], hsem.at[0, p], xh=1 - xh)

    def col_z(p):
        q = piece[p]
        arrived(cols.at[y, co, 1 - xh, q, zp], hsem.at[0, p])
        push(cols.at[y, co, :, q, zp], hsem.at[1, p], zp=1 - zp)

    def col_y(p):
        q = piece[p]
        arrived(cols.at[y, co, :, q, 1 - zp], hsem.at[1, p])
        for h in range(2):
            push(cols.at[y, co, h, q], ysem.at[0, p, h], y=nxt)
            push(cols.at[y, co, 1 - h, q], ysem.at[1, p, 1 - h], y=prv)
        other(y, p)

    def col_far(p):
        q = piece[p]
        arrived(cols.at[prv, co, 0, q], ysem.at[0, p, 0])
        push(cols.at[prv, co, 0, q], ysem.at[0, p, 2], y=nxt)
        arrived(cols.at[nxt, co, 1, q], ysem.at[1, p, 1])
        push(cols.at[nxt, co, 1, q], ysem.at[1, p, 2], y=prv)
        arrived(cols.at[prv, co, 1, q], ysem.at[0, p, 1])
        other(prv, p)
        arrived(cols.at[nxt, co, 0, q], ysem.at[1, p, 0])
        other(nxt, p)

    def col_last(p):
        q = piece[p]
        arrived(cols.at[opp, co, 0, q], ysem.at[0, p, 2])
        arrived(cols.at[opp, co, 1, q], ysem.at[1, p, 2])
        other(opp, p)

    row_start()
    col_x(0)
    col_x(1)
    col_x(2)
    row_step(1)
    col_z(0)
    col_x(3)
    col_z(1)
    col_z(2)
    col_y(0)
    row_step(2)
    col_z(3)
    col_y(1)
    col_y(2)
    col_far(0)
    row_step(3)
    col_y(3)
    col_far(1)
    col_far(2)
    col_last(0)
    row_last()
    col_far(3)
    for p in range(1, 4):
        col_last(p)
    arrived(rows.at[:, :, 1 - xl], xsem)
    arrived(cols.at[:, 1 - co], osem)

    over = (((0,), (0,)), ((), ()))

    def body(i, carry):
        total, late = carry
        r = rows[i // 2, i % 2].reshape(512, 128)
        c = cols[i // 2, i % 2].reshape(512, 256)
        total += lax.dot_general(r, c, over, preferred_element_type=jnp.float32)
        late += lax.dot_general(r[:448], c[64:], over, preferred_element_type=jnp.float32)
        return total, late

    zero = jnp.zeros(inst.shape, jnp.float32)
    total, late = lax.fori_loop(0, 8, body, (zero, zero))
    inst[...] = total / FRAMES
    lagd[...] = late / (FRAMES - LAG)

    for k, copy in enumerate(sends[:8]):
        pl.when(me_k != k)(copy.wait_send)
    for j, copy in enumerate(sends[8:12]):
        mine = jnp.logical_and(own, zz == 4 * co + j)
        pl.when(jnp.logical_not(mine))(copy.wait_send)
    assert len(sends) == NSEND
    for copy in sends[12:]:
        copy.wait_send()


def shards(frames, frequency, phases):
    vmem = pl.BlockSpec(memory_space=pltpu.VMEM)
    hbm = pl.BlockSpec(memory_space=pltpu.HBM)
    dma = pltpu.SemaphoreType.DMA
    tile = jax.ShapeDtypeStruct((128, 256), jnp.float32)
    inst, lagd = pl.pallas_call(
        kernel,
        out_shape=(tile, tile),
        in_specs=[hbm, hbm, vmem],
        out_specs=(vmem, vmem),
        scratch_shapes=[
            pltpu.VMEM(frames.shape, jnp.bfloat16),
            pltpu.VMEM(frequency.shape, jnp.bfloat16),
            pltpu.VMEM((32, 1024), jnp.bfloat16),
            dma((5,)),
            pltpu.VMEM((4, 2, 2, 4, 2, 32, 128), jnp.bfloat16),
            pltpu.VMEM((4, 2, 2, 4, 2, 32, 256), jnp.bfloat16),
            dma((NSEND,)),
            dma((4,)),
            dma((2, 4, 4)),
            dma,
            dma((4,)),
            dma((2, 4)),
            dma((2, 4, 3)),
            dma,
        ],
        compiler_params=pltpu.CompilerParams(collective_id=0, has_side_effects=True, vmem_limit_bytes=VMEM),
    )(frames, frequency, phases[None])
    return inst[None, None], lagd[None, None]


def solution(mesh):
    fine = Mesh(mesh.devices.reshape(SHAPE), AXES)
    tm, feat = AXES[:4], AXES[4:]
    return jax.shard_map(
        shards,
        mesh=fine,
        in_specs=(P(tm, None), P(None, feat), P(feat)),
        out_specs=(P(tm, feat, None, None), P(tm, feat, None, None)),
        check_vma=False,
    )
```

```python
import math

import jax
import jax.numpy as jnp
from jax import lax
from jax.experimental import pallas as pl
from jax.experimental.pallas import tpu as pltpu
from jax.sharding import Mesh, PartitionSpec as P

SCALE = math.sqrt(2.0)
MESH = pl.DeviceIdType.MESH
AXES = ("xl", "zz", "zp", "y", "xh", "co")
SHAPE = (2, 8, 2, 4, 2, 2)
FRAMES, LAG = 4096, 512
NSEND = 99
VMEM = 56_200_000


def kernel(frames, freq, phases, inst, lagd, fbuf, wbuf, feats, ins, rows, cols, send, rsem, zsem, xsem, csem, hsem, ysem, osem):
    xl, zz, zp, y, xh, co = (lax.axis_index(a) for a in AXES)
    par, zq, up = zz % 2, zz // 2, zz // 4
    me_k = zp * 4 + y
    own = jnp.logical_and(jnp.logical_and(xl == xh, co == par), co == up)
    sends = []

    def remote(src, dst, sem, **dev):
        copy = pltpu.make_async_remote_copy(
            src_ref=src,
            dst_ref=dst,
            send_sem=send.at[len(sends)],
            recv_sem=sem,
            device_id=dev,
            device_id_type=MESH,
        )
        sends.append(copy)
        return copy

    def arrived(ref, sem):
        pltpu.make_async_copy(ref, ref, sem).wait()

    barrier = pltpu.get_barrier_semaphore()

    def greet(**dev):
        pl.semaphore_signal(barrier, inc=1, device_id=dev, device_id_type=MESH)

    for q in range(4):
        @pl.when(jnp.logical_not(jnp.logical_and(own, zq == q)))
        def _():
            greet(xl=xh, xh=xl, zz=2 * q + co, co=up)
    for d in range(1, 8):
        k = (me_k + d) % 8
        greet(zp=k // 4, y=k % 4)
    above, below = (zz + 1) % 8, (zz + 7) % 8
    greet(zz=above)
    greet(zz=below)
    greet(xl=1 - xl)
    greet(xh=1 - xh)
    greet(co=1 - co)

    loads = [pltpu.make_async_copy(frames, fbuf, ins.at[4])]
    for j in range(4):
        part = slice(256 * j, 256 * (j + 1))
        loads.append(pltpu.make_async_copy(freq.at[:, part], wbuf.at[:, part], ins.at[j]))
    for load in loads:
        load.start()
    loads[0].wait()
    for j in range(4):
        part = slice(256 * j, 256 * (j + 1))
        loads[1 + j].wait()
        projected = jnp.dot(fbuf[...], wbuf[:, part], preferred_element_type=jnp.float32)
        projected += phases[:, part]
        feats[:, part] = (SCALE * jnp.cos(projected)).astype(jnp.bfloat16)
    pl.semaphore_wait(barrier, 16 - own.astype(jnp.int32))

    for j in range(4):
        src = feats.at[:, 256 * j : 256 * (j + 1)]
        dst = cols.at[y, par, xl, zq, zp]
        mine = jnp.logical_and(own, zz == 4 * co + j)
        copy = remote(src, dst, csem.at[zq], xl=xh, xh=xl, zz=4 * co + j, co=par)
        local = pltpu.make_async_copy(src, dst, csem.at[zq])
        pl.when(jnp.logical_not(mine))(copy.start)
        pl.when(mine)(local.start)
    for k in range(8):
        src = feats.at[:, 128 * k : 128 * (k + 1)]
        dst = rows.at[y, par, xl, zq, zp]
        copy = remote(src, dst, rsem.at[y], zp=k // 4, y=k % 4)
        local = pltpu.make_async_copy(src, dst, rsem.at[y])
        pl.when(me_k != k)(copy.start)
        pl.when(me_k == k)(local.start)

    def push(ref, sem, **dev):
        remote(ref, ref, sem, **dev).start()

    def chunk(z, d):
        return rows.at[(y + d) % 4, z % 2, xl, z // 2]

    def across(z):
        push(rows.at[:, z % 2, xl, z // 2], xsem, xl=1 - xl)

    def row_start():
        for d in range(4):
            v = (y + d) % 4
            arrived(chunk(zz, d), rsem.at[v])
            push(chunk(zz, d), zsem.at[0, 0, d], zz=above)
            push(chunk(zz, d), zsem.at[1, 0, d], zz=below)
        across(zz)

    def row_step(s):
        lo, hi = (zz + 8 - s) % 8, (zz + s) % 8
        for d in range(4):
            arrived(chunk(lo, d), zsem.at[0, s - 1, d])
            if s < 3 or d < 2:
                push(chunk(lo, d), zsem.at[0, s, d], zz=above)
            arrived(chunk(hi, d), zsem.at[1, s - 1, d])
            if s < 3 or d >= 2:
                push(chunk(hi, d), zsem.at[1, s, d], zz=below)
        across(lo)
        across(hi)

    def row_last():
        last = (zz + 4) % 8
        for d in range(4):
            arrived(chunk(last, d), zsem.at[d // 2, 3, d])
            push(chunk(last, d), xsem, xl=1 - xl)

    nxt, prv, opp = (y + 1) % 4, (y + 3) % 4, (y + 2) % 4
    piece = [(zq + d) % 4 for d in (0, 1, 3, 2)]

    def other(d, p):
        push(cols.at[(y + d) % 4, co, :, piece[p]], osem.at[d], co=1 - co)

    def col_x(p):
        q = piece[p]
        arrived(cols.at[y, co, xh, q, zp], csem.at[q])
        push(cols.at[y, co, xh, q, zp], hsem.at[0, p], xh=1 - xh)

    def col_z(p):
        q = piece[p]
        arrived(cols.at[y, co, 1 - xh, q, zp], hsem.at[0, p])
        push(cols.at[y, co, :, q, zp], hsem.at[1, p], zp=1 - zp)

    def col_y(p):
        q = piece[p]
        arrived(cols.at[y, co, :, q, 1 - zp], hsem.at[1, p])
        for h in range(2):
            push(cols.at[y, co, h, q], ysem.at[0, p, h], y=nxt)
            push(cols.at[y, co, 1 - h, q], ysem.at[1, p, 1 - h], y=prv)
        other(0, p)

    def col_far(p):
        q = piece[p]
        arrived(cols.at[prv, co, 0, q], ysem.at[0, p, 0])
        push(cols.at[prv, co, 0, q], ysem.at[0, p, 2], y=nxt)
        arrived(cols.at[nxt, co, 1, q], ysem.at[1, p, 1])
        push(cols.at[nxt, co, 1, q], ysem.at[1, p, 2], y=prv)
        arrived(cols.at[prv, co, 1, q], ysem.at[0, p, 1])
        other(3, p)
        arrived(cols.at[nxt, co, 0, q], ysem.at[1, p, 0])
        other(1, p)

    def col_last(p):
        q = piece[p]
        arrived(cols.at[opp, co, 0, q], ysem.at[0, p, 2])
        arrived(cols.at[opp, co, 1, q], ysem.at[1, p, 2])
        other(2, p)

    row_start()
    for p in range(4):
        col_x(p)
    col_z(0)
    row_step(1)
    col_z(1)
    col_z(2)
    col_y(0)
    col_z(3)
    col_y(1)
    row_step(2)
    col_y(2)
    col_y(3)
    col_far(0)
    col_far(1)
    col_far(2)
    row_step(3)
    col_last(0)
    col_far(3)
    col_last(1)
    row_last()
    col_last(2)
    col_last(3)
    arrived(rows.at[:, :, 1 - xl], xsem)

    over = (((0,), (0,)), ((), ()))

    def add(d, side, carry):
        total, late = carry
        v = (y + d) % 4
        r = rows[v, side].reshape(512, 128)
        c = cols[v, side].reshape(512, 256)
        total += lax.dot_general(r, c, over, preferred_element_type=jnp.float32)
        late += lax.dot_general(r[:448], c[64:], over, preferred_element_type=jnp.float32)
        return total, late

    def others(d, carry):
        arrived(cols.at[(y + d) % 4, 1 - co], osem.at[d])
        return add(d, 1 - co, carry)

    zero = jnp.zeros(inst.shape, jnp.float32)
    sums = lax.fori_loop(0, 4, lambda d, carry: add(d, co, carry), (zero, zero))
    total, late = lax.fori_loop(0, 4, others, sums)
    inst[...] = total / FRAMES
    lagd[...] = late / (FRAMES - LAG)

    for j, copy in enumerate(sends[:4]):
        mine = jnp.logical_and(own, zz == 4 * co + j)
        pl.when(jnp.logical_not(mine))(copy.wait_send)
    for k, copy in enumerate(sends[4:12]):
        pl.when(me_k != k)(copy.wait_send)
    assert len(sends) == NSEND
    for copy in sends[12:]:
        copy.wait_send()


def shards(frames, frequency, phases):
    vmem = pl.BlockSpec(memory_space=pltpu.VMEM)
    hbm = pl.BlockSpec(memory_space=pltpu.HBM)
    dma = pltpu.SemaphoreType.DMA
    tile = jax.ShapeDtypeStruct((128, 256), jnp.float32)
    inst, lagd = pl.pallas_call(
        kernel,
        out_shape=(tile, tile),
        in_specs=[hbm, hbm, vmem],
        out_specs=(vmem, vmem),
        scratch_shapes=[
            pltpu.VMEM(frames.shape, jnp.bfloat16),
            pltpu.VMEM(frequency.shape, jnp.bfloat16),
            pltpu.VMEM((32, 1024), jnp.bfloat16),
            dma((5,)),
            pltpu.VMEM((4, 2, 2, 4, 2, 32, 128), jnp.bfloat16),
            pltpu.VMEM((4, 2, 2, 4, 2, 32, 256), jnp.bfloat16),
            dma((NSEND,)),
            dma((4,)),
            dma((2, 4, 4)),
            dma,
            dma((4,)),
            dma((2, 4)),
            dma((2, 4, 3)),
            dma((4,)),
        ],
        compiler_params=pltpu.CompilerParams(collective_id=0, has_side_effects=True, vmem_limit_bytes=VMEM),
    )(frames, frequency, phases[None])
    return inst[None, None], lagd[None, None]


def solution(mesh):
    fine = Mesh(mesh.devices.reshape(SHAPE), AXES)
    tm, feat = AXES[:4], AXES[4:]
    return jax.shard_map(
        shards,
        mesh=fine,
        in_specs=(P(tm, None), P(None, feat), P(feat)),
        out_specs=(P(tm, feat, None, None), P(tm, feat, None, None)),
        check_vma=False,
    )
```

```python
import math

import jax
import jax.numpy as jnp
from jax import lax
from jax.experimental import pallas as pl
from jax.experimental.pallas import tpu as pltpu
from jax.sharding import Mesh, PartitionSpec as P

SCALE = math.sqrt(2.0)
MESH = pl.DeviceIdType.MESH
AXES = ("xl", "zz", "zp", "y", "xh", "co")
SHAPE = (2, 8, 2, 4, 2, 2)
FRAMES, LAG = 4096, 512
NSEND = 99
VMEM = 56_200_000


def kernel(frames, freq, phases, inst, lagd, fbuf, wbuf, feats, ins, rows, cols, send, rsem, zsem, xsem, csem, hsem, ysem, osem):
    xl, zz, zp, y, xh, co = (lax.axis_index(a) for a in AXES)
    par, zq, up = zz % 2, zz // 2, zz // 4
    me_k = zp * 4 + y
    own = jnp.logical_and(jnp.logical_and(xl == xh, co == par), co == up)
    sends = []

    def remote(src, dst, sem, **dev):
        copy = pltpu.make_async_remote_copy(
            src_ref=src,
            dst_ref=dst,
            send_sem=send.at[len(sends)],
            recv_sem=sem,
            device_id=dev,
            device_id_type=MESH,
        )
        sends.append(copy)
        return copy

    def arrived(ref, sem):
        pltpu.make_async_copy(ref, ref, sem).wait()

    barrier = pltpu.get_barrier_semaphore()

    def greet(**dev):
        pl.semaphore_signal(barrier, inc=1, device_id=dev, device_id_type=MESH)

    for q in range(4):
        @pl.when(jnp.logical_not(jnp.logical_and(own, zq == q)))
        def _():
            greet(xl=xh, xh=xl, zz=2 * q + co, co=up)
    for d in range(1, 8):
        k = (me_k + d) % 8
        greet(zp=k // 4, y=k % 4)
    above, below = (zz + 1) % 8, (zz + 7) % 8
    greet(zz=above)
    greet(zz=below)
    greet(xl=1 - xl)
    greet(xh=1 - xh)
    greet(co=1 - co)

    loads = [pltpu.make_async_copy(frames, fbuf, ins.at[4])]
    for j in range(4):
        part = slice(256 * j, 256 * (j + 1))
        loads.append(pltpu.make_async_copy(freq.at[:, part], wbuf.at[:, part], ins.at[j]))
    for load in loads:
        load.start()
    loads[0].wait()
    for j in range(4):
        part = slice(256 * j, 256 * (j + 1))
        loads[1 + j].wait()
        projected = jnp.dot(fbuf[...], wbuf[:, part], preferred_element_type=jnp.float32)
        projected += phases[:, part]
        feats[:, part] = (SCALE * jnp.cos(projected)).astype(jnp.bfloat16)
    pl.semaphore_wait(barrier, 16 - own.astype(jnp.int32))

    for k in range(8):
        src = feats.at[:, 128 * k : 128 * (k + 1)]
        dst = rows.at[y, par, xl, zq, zp]
        copy = remote(src, dst, rsem.at[y], zp=k // 4, y=k % 4)
        local = pltpu.make_async_copy(src, dst, rsem.at[y])
        pl.when(me_k != k)(copy.start)
        pl.when(me_k == k)(local.start)
    for j in range(4):
        src = feats.at[:, 256 * j : 256 * (j + 1)]
        dst = cols.at[y, par, xl, zq, zp]
        mine = jnp.logical_and(own, zz == 4 * co + j)
        copy = remote(src, dst, csem.at[zq], xl=xh, xh=xl, zz=4 * co + j, co=par)
        local = pltpu.make_async_copy(src, dst, csem.at[zq])
        pl.when(jnp.logical_not(mine))(copy.start)
        pl.when(mine)(local.start)

    def push(ref, sem, **dev):
        remote(ref, ref, sem, **dev).start()

    def chunk(z, d):
        return rows.at[(y + d) % 4, z % 2, xl, z // 2]

    def across(z):
        push(rows.at[:, z % 2, xl, z // 2], xsem, xl=1 - xl)

    def row_start():
        for d in range(4):
            v = (y + d) % 4
            arrived(chunk(zz, d), rsem.at[v])
            push(chunk(zz, d), zsem.at[0, 0, d], zz=above)
            push(chunk(zz, d), zsem.at[1, 0, d], zz=below)
        across(zz)

    def row_step(s):
        lo, hi = (zz + 8 - s) % 8, (zz + s) % 8
        for d in range(4):
            arrived(chunk(lo, d), zsem.at[0, s - 1, d])
            if s < 3 or d < 2:
                push(chunk(lo, d), zsem.at[0, s, d], zz=above)
            arrived(chunk(hi, d), zsem.at[1, s - 1, d])
            if s < 3 or d >= 2:
                push(chunk(hi, d), zsem.at[1, s, d], zz=below)
        across(lo)
        across(hi)

    def row_last():
        last = (zz + 4) % 8
        for d in range(4):
            arrived(chunk(last, d), zsem.at[d // 2, 3, d])
            push(chunk(last, d), xsem, xl=1 - xl)

    nxt, prv, opp = (y + 1) % 4, (y + 3) % 4, (y + 2) % 4
    piece = [(zq + d) % 4 for d in (0, 1, 3, 2)]

    def other(d, p):
        push(cols.at[(y + d) % 4, co, :, piece[p]], osem.at[d], co=1 - co)

    def col_x(p):
        q = piece[p]
        arrived(cols.at[y, co, xh, q, zp], csem.at[q])
        push(cols.at[y, co, xh, q, zp], hsem.at[0, p], xh=1 - xh)

    def col_z(p):
        q = piece[p]
        arrived(cols.at[y, co, 1 - xh, q, zp], hsem.at[0, p])
        push(cols.at[y, co, :, q, zp], hsem.at[1, p], zp=1 - zp)

    def col_y(p):
        q = piece[p]
        arrived(cols.at[y, co, :, q, 1 - zp], hsem.at[1, p])
        for h in range(2):
            push(cols.at[y, co, h, q], ysem.at[0, p, h], y=nxt)
            push(cols.at[y, co, 1 - h, q], ysem.at[1, p, 1 - h], y=prv)
        other(0, p)

    def col_far(p):
        q = piece[p]
        arrived(cols.at[prv, co, 0, q], ysem.at[0, p, 0])
        push(cols.at[prv, co, 0, q], ysem.at[0, p, 2], y=nxt)
        arrived(cols.at[nxt, co, 1, q], ysem.at[1, p, 1])
        push(cols.at[nxt, co, 1, q], ysem.at[1, p, 2], y=prv)
        arrived(cols.at[prv, co, 1, q], ysem.at[0, p, 1])
        other(3, p)
        arrived(cols.at[nxt, co, 0, q], ysem.at[1, p, 0])
        other(1, p)

    def col_last(p):
        q = piece[p]
        arrived(cols.at[opp, co, 0, q], ysem.at[0, p, 2])
        arrived(cols.at[opp, co, 1, q], ysem.at[1, p, 2])
        other(2, p)

    row_start()
    for p in range(4):
        col_x(p)
    row_step(1)
    for p in range(4):
        col_z(p)
    row_step(2)
    for p in range(4):
        col_y(p)
    row_step(3)
    row_last()
    for p in range(4):
        col_far(p)
    for p in range(4):
        col_last(p)
    arrived(rows.at[:, :, 1 - xl], xsem)

    over = (((0,), (0,)), ((), ()))

    def add(d, side, carry):
        total, late = carry
        v = (y + d) % 4
        r = rows[v, side].reshape(512, 128)
        c = cols[v, side].reshape(512, 256)
        total += lax.dot_general(r, c, over, preferred_element_type=jnp.float32)
        late += lax.dot_general(r[:448], c[64:], over, preferred_element_type=jnp.float32)
        return total, late

    def others(d, carry):
        arrived(cols.at[(y + d) % 4, 1 - co], osem.at[d])
        return add(d, 1 - co, carry)

    zero = jnp.zeros(inst.shape, jnp.float32)
    sums = lax.fori_loop(0, 4, lambda d, carry: add(d, co, carry), (zero, zero))
    total, late = lax.fori_loop(0, 4, others, sums)
    inst[...] = total / FRAMES
    lagd[...] = late / (FRAMES - LAG)

    for j, copy in enumerate(sends[8:12]):
        mine = jnp.logical_and(own, zz == 4 * co + j)
        pl.when(jnp.logical_not(mine))(copy.wait_send)
    for k, copy in enumerate(sends[:8]):
        pl.when(me_k != k)(copy.wait_send)
    assert len(sends) == NSEND
    for copy in sends[12:]:
        copy.wait_send()


def shards(frames, frequency, phases):
    vmem = pl.BlockSpec(memory_space=pltpu.VMEM)
    hbm = pl.BlockSpec(memory_space=pltpu.HBM)
    dma = pltpu.SemaphoreType.DMA
    tile = jax.ShapeDtypeStruct((128, 256), jnp.float32)
    inst, lagd = pl.pallas_call(
        kernel,
        out_shape=(tile, tile),
        in_specs=[hbm, hbm, vmem],
        out_specs=(vmem, vmem),
        scratch_shapes=[
            pltpu.VMEM(frames.shape, jnp.bfloat16),
            pltpu.VMEM(frequency.shape, jnp.bfloat16),
            pltpu.VMEM((32, 1024), jnp.bfloat16),
            dma((5,)),
            pltpu.VMEM((4, 2, 2, 4, 2, 32, 128), jnp.bfloat16),
            pltpu.VMEM((4, 2, 2, 4, 2, 32, 256), jnp.bfloat16),
            dma((NSEND,)),
            dma((4,)),
            dma((2, 4, 4)),
            dma,
            dma((4,)),
            dma((2, 4)),
            dma((2, 4, 3)),
            dma((4,)),
        ],
        compiler_params=pltpu.CompilerParams(collective_id=0, has_side_effects=True, vmem_limit_bytes=VMEM),
    )(frames, frequency, phases[None])
    return inst[None, None], lagd[None, None]


def solution(mesh):
    fine = Mesh(mesh.devices.reshape(SHAPE), AXES)
    tm, feat = AXES[:4], AXES[4:]
    return jax.shard_map(
        shards,
        mesh=fine,
        in_specs=(P(tm, None), P(None, feat), P(feat)),
        out_specs=(P(tm, feat, None, None), P(tm, feat, None, None)),
        check_vma=False,
    )
```

```python
import math

import jax
import jax.numpy as jnp
from jax import lax
from jax.experimental import pallas as pl
from jax.experimental.pallas import tpu as pltpu
from jax.sharding import Mesh, PartitionSpec as P

SCALE = math.sqrt(2.0)
MESH = pl.DeviceIdType.MESH
AXES = ("xl", "zz", "zp", "y", "xh", "co")
SHAPE = (2, 8, 2, 4, 2, 2)
FRAMES, LAG = 4096, 512
NSEND = 99
VMEM = 56_200_000


def kernel(frames, freq, phases, inst, lagd, fbuf, wbuf, feats, ins, rows, cols, send, rsem, zsem, xsem, csem, hsem, ysem, osem):
    xl, zz, zp, y, xh, co = (lax.axis_index(a) for a in AXES)
    par, zq, up = zz % 2, zz // 2, zz // 4
    me_k = zp * 4 + y
    own = jnp.logical_and(jnp.logical_and(xl == xh, co == par), co == up)
    sends = []

    def remote(src, dst, sem, **dev):
        copy = pltpu.make_async_remote_copy(
            src_ref=src,
            dst_ref=dst,
            send_sem=send.at[len(sends)],
            recv_sem=sem,
            device_id=dev,
            device_id_type=MESH,
        )
        sends.append(copy)
        return copy

    def arrived(ref, sem):
        pltpu.make_async_copy(ref, ref, sem).wait()

    barrier = pltpu.get_barrier_semaphore()

    def greet(**dev):
        pl.semaphore_signal(barrier, inc=1, device_id=dev, device_id_type=MESH)

    for q in range(4):
        @pl.when(jnp.logical_not(jnp.logical_and(own, zq == q)))
        def _():
            greet(xl=xh, xh=xl, zz=2 * q + co, co=up)
    for d in range(1, 8):
        k = (me_k + d) % 8
        greet(zp=k // 4, y=k % 4)
    above, below = (zz + 1) % 8, (zz + 7) % 8
    greet(zz=above)
    greet(zz=below)
    greet(xl=1 - xl)
    greet(xh=1 - xh)
    greet(co=1 - co)

    loads = [pltpu.make_async_copy(frames, fbuf, ins.at[4])]
    for j in range(4):
        part = slice(256 * j, 256 * (j + 1))
        loads.append(pltpu.make_async_copy(freq.at[:, part], wbuf.at[:, part], ins.at[j]))
    for load in loads:
        load.start()
    loads[0].wait()
    for j in range(4):
        part = slice(256 * j, 256 * (j + 1))
        loads[1 + j].wait()
        projected = jnp.dot(fbuf[...], wbuf[:, part], preferred_element_type=jnp.float32)
        projected += phases[:, part]
        feats[:, part] = (SCALE * jnp.cos(projected)).astype(jnp.bfloat16)
    pl.semaphore_wait(barrier, 16 - own.astype(jnp.int32))

    for k in range(8):
        src = feats.at[:, 128 * k : 128 * (k + 1)]
        dst = rows.at[y, par, xl, zq, zp]
        copy = remote(src, dst, rsem.at[y], zp=k // 4, y=k % 4)
        local = pltpu.make_async_copy(src, dst, rsem.at[y])
        pl.when(me_k != k)(copy.start)
        pl.when(me_k == k)(local.start)
    for j in range(4):
        src = feats.at[:, 256 * j : 256 * (j + 1)]
        dst = cols.at[y, par, xl, zq, zp]
        mine = jnp.logical_and(own, zz == 4 * co + j)
        copy = remote(src, dst, csem.at[zq], xl=xh, xh=xl, zz=4 * co + j, co=par)
        local = pltpu.make_async_copy(src, dst, csem.at[zq])
        pl.when(jnp.logical_not(mine))(copy.start)
        pl.when(mine)(local.start)

    def push(ref, sem, **dev):
        remote(ref, ref, sem, **dev).start()

    def chunk(z, d):
        return rows.at[(y + d) % 4, z % 2, xl, z // 2]

    def across(z):
        push(rows.at[:, z % 2, xl, z // 2], xsem, xl=1 - xl)

    def row_start():
        for d in range(4):
            v = (y + d) % 4
            arrived(chunk(zz, d), rsem.at[v])
            push(chunk(zz, d), zsem.at[0, 0, d], zz=above)
            push(chunk(zz, d), zsem.at[1, 0, d], zz=below)
        across(zz)

    def row_step(s):
        lo, hi = (zz + 8 - s) % 8, (zz + s) % 8
        for d in range(4):
            arrived(chunk(lo, d), zsem.at[0, s - 1, d])
            if s < 3 or d < 2:
                push(chunk(lo, d), zsem.at[0, s, d], zz=above)
            arrived(chunk(hi, d), zsem.at[1, s - 1, d])
            if s < 3 or d >= 2:
                push(chunk(hi, d), zsem.at[1, s, d], zz=below)
        across(lo)
        across(hi)

    def row_last():
        last = (zz + 4) % 8
        for d in range(4):
            arrived(chunk(last, d), zsem.at[d // 2, 3, d])
            push(chunk(last, d), xsem, xl=1 - xl)

    nxt, prv, opp = (y + 1) % 4, (y + 3) % 4, (y + 2) % 4
    piece = [(zq + d) % 4 for d in (0, 1, 3, 2)]

    def other(d, p):
        push(cols.at[(y + d) % 4, co, :, piece[p]], osem.at[d], co=1 - co)

    def col_x(p):
        q = piece[p]
        arrived(cols.at[y, co, xh, q, zp], csem.at[q])
        push(cols.at[y, co, xh, q, zp], hsem.at[0, p], xh=1 - xh)

    def col_z(p):
        q = piece[p]
        arrived(cols.at[y, co, 1 - xh, q, zp], hsem.at[0, p])
        push(cols.at[y, co, :, q, zp], hsem.at[1, p], zp=1 - zp)

    def col_y(p):
        q = piece[p]
        arrived(cols.at[y, co, :, q, 1 - zp], hsem.at[1, p])
        for h in range(2):
            push(cols.at[y, co, h, q], ysem.at[0, p, h], y=nxt)
            push(cols.at[y, co, 1 - h, q], ysem.at[1, p, 1 - h], y=prv)
        other(0, p)

    def col_far(p):
        q = piece[p]
        arrived(cols.at[prv, co, 0, q], ysem.at[0, p, 0])
        push(cols.at[prv, co, 0, q], ysem.at[0, p, 2], y=nxt)
        arrived(cols.at[nxt, co, 1, q], ysem.at[1, p, 1])
        push(cols.at[nxt, co, 1, q], ysem.at[1, p, 2], y=prv)
        arrived(cols.at[prv, co, 1, q], ysem.at[0, p, 1])
        other(3, p)
        arrived(cols.at[nxt, co, 0, q], ysem.at[1, p, 0])
        other(1, p)

    def col_last(p):
        q = piece[p]
        arrived(cols.at[opp, co, 0, q], ysem.at[0, p, 2])
        arrived(cols.at[opp, co, 1, q], ysem.at[1, p, 2])
        other(2, p)

    row_start()
    for p in range(4):
        col_x(p)
    row_step(1)
    for p in range(4):
        col_z(p)
    row_step(2)
    for p in range(4):
        col_y(p)
    row_step(3)
    for p in range(4):
        col_far(p)
    row_last()
    for p in range(4):
        col_last(p)
    arrived(rows.at[:, :, 1 - xl], xsem)

    over = (((0,), (0,)), ((), ()))

    def add(d, side, carry):
        total, late = carry
        v = (y + d) % 4
        r = rows[v, side].reshape(512, 128)
        c = cols[v, side].reshape(512, 256)
        total += lax.dot_general(r, c, over, preferred_element_type=jnp.float32)
        late += lax.dot_general(r[:448], c[64:], over, preferred_element_type=jnp.float32)
        return total, late

    def others(d, carry):
        arrived(cols.at[(y + d) % 4, 1 - co], osem.at[d])
        return add(d, 1 - co, carry)

    zero = jnp.zeros(inst.shape, jnp.float32)
    sums = lax.fori_loop(0, 4, lambda d, carry: add(d, co, carry), (zero, zero))
    total, late = lax.fori_loop(0, 4, others, sums)
    inst[...] = total / FRAMES
    lagd[...] = late / (FRAMES - LAG)

    for j, copy in enumerate(sends[8:12]):
        mine = jnp.logical_and(own, zz == 4 * co + j)
        pl.when(jnp.logical_not(mine))(copy.wait_send)
    for k, copy in enumerate(sends[:8]):
        pl.when(me_k != k)(copy.wait_send)
    assert len(sends) == NSEND
    for copy in sends[12:]:
        copy.wait_send()


def shards(frames, frequency, phases):
    vmem = pl.BlockSpec(memory_space=pltpu.VMEM)
    hbm = pl.BlockSpec(memory_space=pltpu.HBM)
    dma = pltpu.SemaphoreType.DMA
    tile = jax.ShapeDtypeStruct((128, 256), jnp.float32)
    inst, lagd = pl.pallas_call(
        kernel,
        out_shape=(tile, tile),
        in_specs=[hbm, hbm, vmem],
        out_specs=(vmem, vmem),
        scratch_shapes=[
            pltpu.VMEM(frames.shape, jnp.bfloat16),
            pltpu.VMEM(frequency.shape, jnp.bfloat16),
            pltpu.VMEM((32, 1024), jnp.bfloat16),
            dma((5,)),
            pltpu.VMEM((4, 2, 2, 4, 2, 32, 128), jnp.bfloat16),
            pltpu.VMEM((4, 2, 2, 4, 2, 32, 256), jnp.bfloat16),
            dma((NSEND,)),
            dma((4,)),
            dma((2, 4, 4)),
            dma,
            dma((4,)),
            dma((2, 4)),
            dma((2, 4, 3)),
            dma((4,)),
        ],
        compiler_params=pltpu.CompilerParams(collective_id=0, has_side_effects=True, vmem_limit_bytes=VMEM),
    )(frames, frequency, phases[None])
    return inst[None, None], lagd[None, None]


def solution(mesh):
    fine = Mesh(mesh.devices.reshape(SHAPE), AXES)
    tm, feat = AXES[:4], AXES[4:]
    return jax.shard_map(
        shards,
        mesh=fine,
        in_specs=(P(tm, None), P(None, feat), P(feat)),
        out_specs=(P(tm, feat, None, None), P(tm, feat, None, None)),
        check_vma=False,
    )
```
